32 devices in a mesh: ctx: 8 (over z, y), fsdp: 4 (over x, core).
Axes of the slice: x: 2, y: 2, z: 4, core: 2. Of those that a mesh axis runs over, the one named last changes fastest.
Arguments:
- tokens: bfloat16 [4, 1024, 1024], P('fsdp', 'ctx'), may hold values from -6 to 6
- routes: int32 [4, 1024, 8], P('fsdp', 'ctx'), may hold values from 0 to 31, all different within a row; in each aligned block of 128 rows (0 to 127, 128 to 255, ..., all dimensions but the last counted through in order) at most 48 rows name the same one
- route_gates: float32 [4, 1024, 8], P('fsdp', 'ctx'), may hold values from 0.05 to 0.5
- first_gain: bfloat16 [1024], P(('ctx', 'fsdp')), may hold values from 0.099609375 to 1.8984375
- query_weight: bfloat16 [1024, 1024], P(('ctx', 'fsdp')), may hold values from -0.1875 to 0.1875
- key_weight: bfloat16 [1024, 512], P(('ctx', 'fsdp')), may hold values from -0.1875 to 0.1875
- value_matrix: bfloat16 [1024, 512], P(('ctx', 'fsdp')), may hold values from -0.1875 to 0.1875
- output_weight: bfloat16 [1024, 1024], P(('ctx', 'fsdp')), may hold values from -1.5 to 1.5
- second_gain: bfloat16 [1024], P(('ctx', 'fsdp')), may hold values from 0.099609375 to 1.8984375
- expert_gate: bfloat16 [32, 1024, 512], P('ctx', 'fsdp'), may hold values from -0.1875 to 0.1875
- expert_up: bfloat16 [32, 1024, 512], P('ctx', 'fsdp'), may hold values from -0.1875 to 0.1875
- expert_down: bfloat16 [32, 512, 1024], P('ctx', None, 'fsdp'), may hold values from -0.25 to 0.25
- cotangent: bfloat16 [4, 1024, 1024], P('fsdp', 'ctx'), may hold values from -6 to 6
Outputs:
- block_output: bfloat16 [4, 1024, 1024], P('fsdp', 'ctx')
- input_grad: float32 [4, 1024, 1024], P('fsdp', 'ctx')
- first_gain_grad: float32 [1024], P(('ctx', 'fsdp'))
- query_grad: float32 [1024, 1024], P(('ctx', 'fsdp'))
- key_grad: float32 [1024, 512], P(('ctx', 'fsdp'))
- value_grad: float32 [1024, 512], P(('ctx', 'fsdp'))
- output_grad: float32 [1024, 1024], P(('ctx', 'fsdp'))
- second_gain_grad: float32 [1024], P(('ctx', 'fsdp'))
- expert_gate_grad: float32 [32, 1024, 512], P('ctx', 'fsdp')
- expert_up_grad: float32 [32, 1024, 512], P('ctx', 'fsdp')
- expert_down_grad: float32 [32, 512, 1024], P('ctx', None, 'fsdp')
The draws below stay inside these ranges and needn't reach their ends.
Inputs may be any that keep to these rules, and one draw needn't show every extreme that they name: `routes`: within the rows of one device (aligned blocks of 128 rows), no expert is named by more than 48 rows, a bound that some block reaches.
All inputs are finite; a program needn't handle non-finite values.
Results may differ from the reference program's by a relative error of at most 0.017.
Values may be sent and summed in bfloat16 or wider, within the bound.
No kernel may reach another device: no remote copies, remote signals or barrier semaphores. Data moves between devices by JAX's collectives and lax.ppermute only.
A program may use at most 192 MiB of HBM per device.

```python
import math
import jax
import jax.numpy as jnp
import numpy as np
from jax import lax

MODEL_WIDTH = 1024
QUERY_HEADS = 16
KEY_VALUE_HEADS = 8
HEAD_SIZE = 64
NE = 32
FE = 512
TOPK = 8
TOK_DEV = 128
LEN = 1024
SEQS = 4
CAP = 48
N_CTX = 8


def block_levels(own_key, dims, shards, least, largest):
    loudness = 1.0
    for position, parts in shards:
        steps = jax.random.uniform(jax.random.fold_in(jax.random.fold_in(own_key, 6), position), (parts,), jnp.float32, least / len(shards), largest / len(shards))
        loudness = loudness * jnp.repeat(jnp.exp(steps), dims[position] // parts).reshape((-1,) + (1,) * (len(dims) - 1 - position))
    return loudness


def assign_block(key, own, number, rows, amount, top, reach, slope):
    order = jax.random.permutation(key, amount)
    crowded, usual = portions_of(amount, rows * top, reach, slope, True), portions_of(amount, rows * top, reach, slope, False)
    places = jnp.arange(amount)

    def named(tallies, rotation):
        used = int((tallies > 0).sum())
        fixed = max(1, used // 4)
        passed = fixed + (places - fixed + rotation * (used - fixed)) % max(1, amount - fixed)
        return jnp.zeros((amount,), jnp.int32).at[order[jnp.where(places < fixed, places, passed)]].set(jnp.asarray(tallies, jnp.int32))

    tallies = jnp.where(number % 4 == 0, named(crowded, number // 4), named(usual, number - number // 4 - 1))
    mixed = jax.random.permutation(jax.random.fold_in(own, 3), amount)
    source_of, taker = mixed[0:amount // 2 * 2:2], mixed[1:amount // 2 * 2:2]
    room = jnp.minimum(tallies[source_of] - 1, reach - tallies[taker]) // 2
    room = jnp.where((source_of == order[0]) | (taker == order[0]) | (tallies[taker] == 0), 0, jnp.maximum(room, 0))
    passed = jax.random.randint(jax.random.fold_in(own, 4), (amount // 2,), 0, 1 << 20) % (room + 1)
    tallies = tallies.at[source_of].add(-passed).at[taker].add(passed)
    members = jnp.searchsorted(jnp.cumsum(tallies), jnp.arange(rows * top), side="right").astype(jnp.int32)
    grid = members.reshape(top, rows).T
    grid = grid[jax.random.permutation(jax.random.fold_in(own, 1), rows)]
    rotation = jax.random.randint(jax.random.fold_in(own, 2), (rows, 1), 0, top)
    return jnp.take_along_axis(grid, (jnp.arange(top)[None, :] + rotation) % top, axis=1)


def portions_of(count, total, most, slope, full):
    weights = [(1 << 20) // math.isqrt(grade ** slope) + 1 for grade in range(1, count + 1)]
    largest = most if full else min(most, max(-(-total // count), total * weights[0] // sum(weights)))
    least = 1 if total - largest >= count - 1 else 0
    counts, surplus = [largest] + [least] * (count - 1), total - largest - least * (count - 1)
    while surplus > 0:
        candidates = [i for i in range(1, count) if counts[i] < largest] or [i for i in range(1, count) if counts[i] < most]
        mass, remaining = sum([weights[i] for i in candidates]), surplus
        for i in candidates:
            addition = min(most - counts[i], max(1, remaining * weights[i] // mass), surplus)
            counts[i] = counts[i] + addition
            surplus = surplus - addition
    return np.array(counts)


def normal_values(stream_key, extent, width, most, split=(), kind=jnp.bfloat16):
    values = width * jax.random.normal(stream_key, extent, jnp.float32)
    if split:
        values = values * block_levels(stream_key, extent, split, -0.22, 0.18)
    return jnp.clip(values, -most, most).astype(kind)


def setup_inputs(seed: int = 0) -> dict:
    arg_keys = jax.random.split(jax.random.key(seed), 14)
    tokens = normal_values(arg_keys[0], (SEQS, LEN, MODEL_WIDTH), 1.0, 6.0, ((0, 4), (1, 8)))
    routes_keys = jax.random.split(jax.random.fold_in(arg_keys[1], 1), SEQS * LEN // TOK_DEV)
    routes_turns = jax.random.permutation(jax.random.fold_in(arg_keys[1], 3), SEQS * LEN // TOK_DEV)
    routes = jax.vmap(lambda own, number: assign_block(jax.random.fold_in(arg_keys[1], 2), own, number, TOK_DEV, NE, TOPK, CAP, 1))(routes_keys, routes_turns).reshape((SEQS, LEN, TOPK))
    route_gates = jnp.clip(jnp.exp(math.log(0.5) - 2.3025851 * jax.random.uniform(arg_keys[2], (SEQS, LEN, TOPK), jnp.float32) ** block_levels(arg_keys[2], (SEQS, LEN, TOPK), ((0, 4), (1, 8)), -0.2, 0.2)), 0.05, 0.5)
    first_gain = jnp.clip(1.0 + 0.18 * jax.random.normal(arg_keys[3], (MODEL_WIDTH,), jnp.float32), 0.099609375, 1.8984375).astype(jnp.bfloat16)
    query_weight = normal_values(arg_keys[4], (MODEL_WIDTH, QUERY_HEADS * HEAD_SIZE), MODEL_WIDTH ** -0.5, 0.1875, ((0, 32),))
    key_weight = normal_values(arg_keys[5], (MODEL_WIDTH, KEY_VALUE_HEADS * HEAD_SIZE), MODEL_WIDTH ** -0.5, 0.1875, ((0, 32),))
    value_matrix = normal_values(arg_keys[6], (MODEL_WIDTH, KEY_VALUE_HEADS * HEAD_SIZE), MODEL_WIDTH ** -0.5, 0.1875, ((0, 32),))
    output_weight = normal_values(arg_keys[7], (QUERY_HEADS * HEAD_SIZE, MODEL_WIDTH), (QUERY_HEADS * HEAD_SIZE // 64) ** -0.5, 1.5, ((0, 32),))
    second_gain = jnp.clip(1.0 + 0.18 * jax.random.normal(arg_keys[8], (MODEL_WIDTH,), jnp.float32), 0.099609375, 1.8984375).astype(jnp.bfloat16)
    expert_gate = normal_values(arg_keys[9], (NE, MODEL_WIDTH, FE), MODEL_WIDTH ** -0.5, 0.1875, ((0, 8), (1, 4)))
    expert_up = normal_values(arg_keys[10], (NE, MODEL_WIDTH, FE), MODEL_WIDTH ** -0.5, 0.1875, ((0, 8), (1, 4)))
    expert_down = normal_values(arg_keys[11], (NE, FE, MODEL_WIDTH), FE ** -0.5, 0.25, ((0, 8), (2, 4)))
    cotangent = normal_values(arg_keys[12], (SEQS, LEN, MODEL_WIDTH), 1.0, 6.0, ((0, 4), (1, 8)))
    return dict(tokens=tokens, routes=routes, route_gates=route_gates, first_gain=first_gain, query_weight=query_weight, key_weight=key_weight, value_matrix=value_matrix, output_weight=output_weight, second_gain=second_gain, expert_gate=expert_gate, expert_up=expert_up, expert_down=expert_down, cotangent=cotangent)


EPSILON = 1e-05
ROPE_BASE = 10000.0

def positions(index, count_of_rows, ctx_count):
    block = index // count_of_rows
    local = index % count_of_rows
    half = count_of_rows // 2
    return jnp.where(local < half, block * half + local, (2 * ctx_count - 1 - block) * half + local - half)

def rotary(places):
    freqs = ROPE_BASE ** (-jnp.arange(0, HEAD_SIZE, 2, dtype=jnp.float32) / HEAD_SIZE)
    angles = places.astype(jnp.float32)[:, None] * freqs[None, :]
    return (jnp.cos(angles), jnp.sin(angles))

def apply_rotation(values, cosine_table, sine_table):
    half = values.shape[-1] // 2
    first = values[..., :half]
    second = values[..., half:]
    cos_part = cosine_table[:, None, :]
    sin_part = sine_table[:, None, :]
    return jnp.concatenate([first * cos_part - second * sin_part, second * cos_part + first * sin_part], -1)

def as_float(array):
    return array.astype(jnp.float32)

def attend(queries, key_block, value_block, allowed):
    scores = jnp.einsum('qhgd,khd->hgqk', as_float(queries), as_float(key_block)) * HEAD_SIZE ** (-0.5)
    scores = jnp.where(allowed[None, None], scores, -jnp.inf)
    row_peak = lax.optimization_barrier(jnp.max(scores, -1, keepdims=True))
    logsum = row_peak + jnp.log(lax.optimization_barrier(jnp.sum(jnp.exp(scores - row_peak), -1, keepdims=True)))
    prob_rows = jnp.exp(scores - logsum).astype(jnp.bfloat16)
    rows_mixed = jnp.einsum('hgqk,khd->qhgd', as_float(prob_rows), as_float(value_block))
    return (rows_mixed, logsum[..., 0])

def attend_back(queries, key_block, value_block, grad_block, logsum, rows_of_delta, allowed):
    scores = jnp.einsum('qhgd,khd->hgqk', as_float(queries), as_float(key_block)) * HEAD_SIZE ** (-0.5)
    scores = jnp.where(allowed[None, None], scores, -jnp.inf)
    prob_rows = jnp.exp(scores - logsum[..., None])
    grad_probs = jnp.einsum('qhgd,khd->hgqk', as_float(grad_block), as_float(value_block))
    grad_scores = (prob_rows * (grad_probs - rows_of_delta[..., None])).astype(jnp.bfloat16)
    prob_half = prob_rows.astype(jnp.bfloat16)
    grad_queries = jnp.einsum('hgqk,khd->qhgd', as_float(grad_scores), as_float(key_block)) * HEAD_SIZE ** (-0.5)
    grad_keys = jnp.einsum('hgqk,qhgd->khd', as_float(grad_scores), as_float(queries)) * HEAD_SIZE ** (-0.5)
    value_gradient_rows = jnp.einsum('hgqk,qhgd->khd', as_float(prob_half), as_float(grad_block))
    return (grad_queries, grad_keys, value_gradient_rows)

def expert_block(normed_rows, route_rows, weight_rows, upstream_rows, gate_full, up_full, down_full):
    count_of_rows = normed_rows.shape[0]
    route_flat = route_rows.reshape(-1)
    owners = jnp.arange(count_of_rows * TOPK, dtype=jnp.int32) // TOPK
    one_hot = (route_flat[:, None] == jnp.arange(NE, dtype=jnp.int32)[None, :]).astype(jnp.int32)
    slot_index = route_flat * CAP + lax.optimization_barrier(jnp.sum((jnp.cumsum(one_hot, 0) - 1) * one_hot, 1))
    send_rows = jnp.zeros((NE * CAP, MODEL_WIDTH), jnp.bfloat16).at[slot_index].set(normed_rows[owners]).reshape(NE, CAP, MODEL_WIDTH)
    route_cot = (weight_rows.reshape(-1)[:, None] * upstream_rows[owners]).astype(jnp.bfloat16)
    send_grads = jnp.zeros((NE * CAP, MODEL_WIDTH), jnp.bfloat16).at[slot_index].set(route_cot).reshape(NE, CAP, MODEL_WIDTH)
    pre_gate = jnp.einsum('esd,edf->esf', as_float(send_rows), as_float(gate_full))
    pre_up = jnp.einsum('esd,edf->esf', as_float(send_rows), as_float(up_full))
    sigmoid_gate = jax.nn.sigmoid(pre_gate)
    silu_gate = pre_gate * sigmoid_gate
    hidden = (silu_gate * pre_up).astype(jnp.bfloat16)
    expert_out = jnp.einsum('esf,efd->esd', as_float(hidden), as_float(down_full)).astype(jnp.bfloat16)
    grad_hidden = jnp.einsum('esd,efd->esf', as_float(send_grads), as_float(down_full))
    down_grad = jnp.einsum('esf,esd->efd', as_float(hidden), as_float(send_grads))
    grad_pre_gate = (grad_hidden * pre_up * sigmoid_gate * (1.0 + pre_gate * (1.0 - sigmoid_gate))).astype(jnp.bfloat16)
    grad_pre_up = (grad_hidden * silu_gate).astype(jnp.bfloat16)
    gate_grad = jnp.einsum('esd,esf->edf', as_float(send_rows), as_float(grad_pre_gate))
    up_grad = jnp.einsum('esd,esf->edf', as_float(send_rows), as_float(grad_pre_up))
    back_rows = (jnp.einsum('esf,edf->esd', as_float(grad_pre_gate), as_float(gate_full)) + jnp.einsum('esf,edf->esd', as_float(grad_pre_up), as_float(up_full))).astype(jnp.bfloat16)
    picked_out = as_float(expert_out.reshape(NE * CAP, MODEL_WIDTH)[slot_index]).reshape(count_of_rows, TOPK, MODEL_WIDTH)
    expert_sum = lax.optimization_barrier(jnp.sum(weight_rows[:, :, None] * picked_out, 1))
    grad_two = lax.optimization_barrier(jnp.sum(as_float(back_rows.reshape(NE * CAP, MODEL_WIDTH)[slot_index]).reshape(count_of_rows, TOPK, MODEL_WIDTH), 1))
    return (expert_sum, grad_two, gate_grad, up_grad, down_grad)

def reference(tokens, routes, route_gates, first_gain, query_weight, key_weight, value_matrix, output_weight, second_gain, expert_gate, expert_up, expert_down, cotangent):
    sequence_length = tokens.shape[1]
    head_groups = QUERY_HEADS // KEY_VALUE_HEADS
    places = positions(jnp.arange(sequence_length, dtype=jnp.int32), TOK_DEV, N_CTX)
    cosine_table, sine_table = rotary(places)
    allowed = places[None, :] <= places[:, None]
    rows_per_block = min(512, sequence_length)
    count_of_blocks = sequence_length // rows_per_block
    allowed_blocks = allowed.reshape(count_of_blocks, rows_per_block, sequence_length)
    gain_first = first_gain.astype(jnp.float32)
    gain_second = second_gain.astype(jnp.float32)

    def one_sequence(totals, sequence):
        seq_tokens, seq_routes, seq_gates, seq_cot = sequence
        inputs = seq_tokens.astype(jnp.float32)
        scale_one = lax.rsqrt(lax.optimization_barrier(jnp.mean(inputs * inputs, -1, keepdims=True)) + EPSILON)
        unit_one = inputs * scale_one
        normed_one = (unit_one * gain_first).astype(jnp.bfloat16)
        rows_of_query = jnp.dot(normed_one, query_weight, preferred_element_type=jnp.float32)
        rows_of_key = jnp.dot(normed_one, key_weight, preferred_element_type=jnp.float32)
        rows_of_value = jnp.dot(normed_one, value_matrix, preferred_element_type=jnp.float32)
        rotated_query = apply_rotation(rows_of_query.reshape(sequence_length, QUERY_HEADS, HEAD_SIZE), cosine_table, sine_table).astype(jnp.bfloat16).reshape(sequence_length, KEY_VALUE_HEADS, head_groups, HEAD_SIZE)
        rotated_key = apply_rotation(rows_of_key.reshape(sequence_length, KEY_VALUE_HEADS, HEAD_SIZE), cosine_table, sine_table).astype(jnp.bfloat16)
        heads_of_value = rows_of_value.astype(jnp.bfloat16).reshape(sequence_length, KEY_VALUE_HEADS, HEAD_SIZE)
        blocks_of_query = rotated_query.reshape(count_of_blocks, rows_per_block, KEY_VALUE_HEADS, head_groups, HEAD_SIZE)

        def forward_block(pair):
            return attend(pair[0], rotated_key, heads_of_value, pair[1])
        mixed_blocks, logsum = lax.map(forward_block, (blocks_of_query, allowed_blocks))
        rows_mixed = mixed_blocks.reshape(sequence_length, QUERY_HEADS * HEAD_SIZE).astype(jnp.bfloat16)
        residual = inputs + jnp.dot(rows_mixed, output_weight, preferred_element_type=jnp.float32)
        scale_two = lax.rsqrt(lax.optimization_barrier(jnp.mean(residual * residual, -1, keepdims=True)) + EPSILON)
        unit_two = residual * scale_two
        normed_two = (unit_two * gain_second).astype(jnp.bfloat16)
        upstream = seq_cot.astype(jnp.float32)

        def expert_step(inner, rows_item):
            expert_sum, grad_two, gate_grad, up_grad, down_grad = expert_block(rows_item[0], rows_item[1], rows_item[2], rows_item[3], expert_gate, expert_up, expert_down)
            return ((inner[0] + gate_grad, inner[1] + up_grad, inner[2] + down_grad), (expert_sum, grad_two))
        expert_totals, (expert_sums, grad_twos) = lax.scan(expert_step, (totals[6], totals[7], totals[8]), (normed_two.reshape(N_CTX, TOK_DEV, MODEL_WIDTH), seq_routes.reshape(N_CTX, TOK_DEV, TOPK), seq_gates.reshape(N_CTX, TOK_DEV, TOPK), upstream.reshape(N_CTX, TOK_DEV, MODEL_WIDTH)))
        expert_sum = expert_sums.reshape(sequence_length, MODEL_WIDTH)
        grad_two = grad_twos.reshape(sequence_length, MODEL_WIDTH)
        block_output = (residual + expert_sum).astype(jnp.bfloat16)
        second_part = lax.optimization_barrier(jnp.sum(grad_two * unit_two, 0))
        scaled_two = grad_two * gain_second
        grad_residual = upstream + scale_two * (scaled_two - unit_two * lax.optimization_barrier(jnp.mean(scaled_two * unit_two, -1, keepdims=True)))
        grad_resid_b = grad_residual.astype(jnp.bfloat16)
        output_part = jnp.dot(rows_mixed.T, grad_resid_b, preferred_element_type=jnp.float32)
        mixed_gradient = jnp.dot(grad_resid_b, output_weight.T, preferred_element_type=jnp.float32).astype(jnp.bfloat16)
        gradient_heads = mixed_gradient.reshape(sequence_length, KEY_VALUE_HEADS, head_groups, HEAD_SIZE)
        rows_of_delta = lax.optimization_barrier(jnp.sum(gradient_heads.astype(jnp.float32) * rows_mixed.reshape(sequence_length, KEY_VALUE_HEADS, head_groups, HEAD_SIZE).astype(jnp.float32), -1))
        blocks_of_delta = rows_of_delta.reshape(count_of_blocks, rows_per_block, KEY_VALUE_HEADS, head_groups).transpose(0, 2, 3, 1)
        gradient_blocks = gradient_heads.reshape(count_of_blocks, rows_per_block, KEY_VALUE_HEADS, head_groups, HEAD_SIZE)

        def back_step(sums, block_item):
            grad_queries, grad_keys, value_gradient_rows = attend_back(block_item[0], rotated_key, heads_of_value, block_item[1], block_item[2], block_item[3], block_item[4])
            return ((sums[0] + grad_keys, sums[1] + value_gradient_rows), grad_queries)
        empty_keys = jnp.zeros((sequence_length, KEY_VALUE_HEADS, HEAD_SIZE), jnp.float32)
        (rotated_key_gradient, value_gradient_rows), grad_query_rot = lax.scan(back_step, (empty_keys, empty_keys), (blocks_of_query, gradient_blocks, logsum, blocks_of_delta, allowed_blocks))
        grad_query = apply_rotation(grad_query_rot.reshape(sequence_length, QUERY_HEADS, HEAD_SIZE), cosine_table, -sine_table).reshape(sequence_length, QUERY_HEADS * HEAD_SIZE).astype(jnp.bfloat16)
        key_gradient = apply_rotation(rotated_key_gradient, cosine_table, -sine_table).reshape(sequence_length, KEY_VALUE_HEADS * HEAD_SIZE).astype(jnp.bfloat16)
        value_gradient = value_gradient_rows.reshape(sequence_length, KEY_VALUE_HEADS * HEAD_SIZE).astype(jnp.bfloat16)
        grad_one = jnp.dot(grad_query, query_weight.T, preferred_element_type=jnp.float32) + jnp.dot(key_gradient, key_weight.T, preferred_element_type=jnp.float32) + jnp.dot(value_gradient, value_matrix.T, preferred_element_type=jnp.float32)
        first_part = lax.optimization_barrier(jnp.sum(grad_one * unit_one, 0))
        scaled_one = grad_one * gain_first
        input_grad = grad_residual + scale_one * (scaled_one - unit_one * lax.optimization_barrier(jnp.mean(scaled_one * unit_one, -1, keepdims=True)))
        query_part = jnp.dot(normed_one.T, grad_query, preferred_element_type=jnp.float32)
        key_part = jnp.dot(normed_one.T, key_gradient, preferred_element_type=jnp.float32)
        value_part = jnp.dot(normed_one.T, value_gradient, preferred_element_type=jnp.float32)
        new_totals = (totals[0] + first_part, totals[1] + query_part, totals[2] + key_part, totals[3] + value_part, totals[4] + output_part, totals[5] + second_part, expert_totals[0], expert_totals[1], expert_totals[2])
        return (new_totals, (block_output, input_grad))
    zero_totals = (jnp.zeros((MODEL_WIDTH,), jnp.float32), jnp.zeros(query_weight.shape, jnp.float32), jnp.zeros(key_weight.shape, jnp.float32), jnp.zeros(value_matrix.shape, jnp.float32), jnp.zeros(output_weight.shape, jnp.float32), jnp.zeros((MODEL_WIDTH,), jnp.float32), jnp.zeros(expert_gate.shape, jnp.float32), jnp.zeros(expert_up.shape, jnp.float32), jnp.zeros(expert_down.shape, jnp.float32))
    totals, (outputs, input_grads) = lax.scan(one_sequence, zero_totals, (tokens, routes, route_gates, cotangent))
    return (outputs, input_grads, totals[0], totals[1], totals[2], totals[3], totals[4], totals[5], totals[6], totals[7], totals[8])
```

```python
import functools

import jax
import jax.numpy as jnp
from jax import lax
from jax.experimental import pallas as pl
from jax.experimental.pallas import tpu as pltpu
from jax.sharding import PartitionSpec as P

MODEL_WIDTH = 1024
QUERY_HEADS = 16
KEY_VALUE_HEADS = 8
HEAD_SIZE = 64
NE = 32
TOPK = 8
CAP = 48


EPSILON = 1e-05
ROPE_BASE = 10000.0
F32 = jnp.float32
BF16 = jnp.bfloat16
VMEM_LIMIT = 60 * 1024 * 1024


def dot_nn(a, b):
    return lax.dot_general(a, b, (((1,), (0,)), ((), ())), preferred_element_type=F32)


def dot_nt(a, b):
    return lax.dot_general(a, b, (((1,), (1,)), ((), ())), preferred_element_type=F32)


def dot_tn(a, b):
    return lax.dot_general(a, b, (((0,), (0,)), ((), ())), preferred_element_type=F32)


def ring_order(n):
    return list(range(0, n, 2)) + list(range(n - 1, 0, -2))


def shift(x, n, by):
    order = ring_order(n)
    return lax.ppermute(x, "ctx", [(order[i], order[(i + by) % n]) for i in range(n)])


def swap(x, bit):
    return lax.ppermute(x, "fsdp", [(i, i ^ bit) for i in range(4)])


def ring_gather(x, n):
    half = n // 2
    result = [None] * n
    result[0] = down = up = x
    for step in range(1, half):
        down, up = shift(down, n, 1), shift(up, n, -1)
        result[n - step], result[step] = down, up
    rows = x.shape[0] // 2
    result[half] = jnp.concatenate([shift(down[:rows], n, 1), shift(up[rows:], n, -1)], 0)
    return result


def ring_scatter(parts, n):
    half = n // 2
    rows = parts[0].shape[0] // 2
    low = shift(parts[half][:rows], n, 1)
    high = shift(parts[half][rows:], n, -1)
    a, b = parts[half - 1], parts[half + 1]
    down = jnp.concatenate([(a[:rows].astype(F32) + low.astype(F32)).astype(BF16), a[rows:]], 0)
    up = jnp.concatenate([b[:rows], (b[rows:].astype(F32) + high.astype(F32)).astype(BF16)], 0)
    for step in range(half - 1, 0, -1):
        down, up = shift(down, n, 1), shift(up, n, -1)
        if step > 1:
            down = (down.astype(F32) + parts[step - 1].astype(F32)).astype(BF16)
            up = (up.astype(F32) + parts[n - step + 1].astype(F32)).astype(BF16)
    return down.astype(F32) + up.astype(F32) + parts[0].astype(F32)


def swap_gather(x):
    across = swap(x, 2)
    return [x, swap(x, 1), across, swap(across, 1)]


def swap_scatter(pieces):
    one, three = swap(pieces[1], 1), swap(pieces[3], 1)
    mine = pieces[0].astype(F32) + one.astype(F32)
    other = (pieces[2].astype(F32) + three.astype(F32)).astype(BF16)
    return mine + swap(other, 2).astype(F32)


def swap_halves(x):
    lane = lax.broadcasted_iota(jnp.int32, x.shape, 1)
    width = x.shape[1]
    quarter = HEAD_SIZE // 2
    return jnp.where(
        lane % HEAD_SIZE < quarter,
        pltpu.roll(x, width - quarter, 1),
        pltpu.roll(x, quarter, 1),
    )


def attention_forward_kernel(
    offs, tok, weight, gain, cos_ref, sin_ref, mixed_ref, normed_ref, qkv_ref, lse_ref, raw, mix
):
    rows = tok.shape[0]
    block = 128
    half = block // 2

    def project(j, _):
        x = tok[pl.ds(j * block, block), :].astype(F32)
        scale = lax.rsqrt(jnp.mean(x * x, -1, keepdims=True) + EPSILON)
        normed = (x * scale * gain[...]).astype(BF16)
        y = dot_nn(normed, weight[...])
        for h in range(2):
            place = pl.multiple_of(offs[2 * j + h], half)
            normed_ref[pl.ds(place, half), :] = normed[h * half : (h + 1) * half]
            raw[pl.ds(place, half), :] = y[h * half : (h + 1) * half]
        return 0

    lax.fori_loop(0, rows // block, project, 0)
    tile = 256

    def rotate(i, _):
        here = pl.ds(pl.multiple_of(i * tile, tile), tile)
        c, s = cos_ref[here, :], sin_ref[here, :]
        q, k = raw[here, 0:128], raw[here, 128:256]
        q = (q * c + swap_halves(q) * s).astype(BF16)
        qkv_ref[here, 0:128] = (q.astype(F32) * HEAD_SIZE ** (-0.5)).astype(BF16)
        qkv_ref[here, 128:256] = (k * c + swap_halves(k) * s).astype(BF16)
        qkv_ref[here, 256:384] = raw[here, 256:384].astype(BF16)
        return 0

    lax.fori_loop(0, rows // tile, rotate, 0)
    lane = lax.broadcasted_iota(jnp.int32, (tile, 128), 1)
    for i in range(rows // tile):
        width = (i + 1) * tile
        here = slice(i * tile, (i + 1) * tile)
        q = qkv_ref[here, 0:128]
        k, v = qkv_ref[0:width, 128:256], qkv_ref[0:width, 256:384]
        row = lax.broadcasted_iota(jnp.int32, (tile, width), 0) + i * tile
        col = lax.broadcasted_iota(jnp.int32, (tile, width), 1)
        outs, sums = [], []
        for h in range(2):
            mask = (lane < HEAD_SIZE) if h == 0 else (lane >= HEAD_SIZE)
            scores = dot_nt(jnp.where(mask, q, jnp.zeros_like(q)), k)
            scores = jnp.where(col <= row, scores, -jnp.inf)
            peak = jnp.max(scores, -1, keepdims=True)
            weights = jnp.exp(scores - peak)
            total = jnp.sum(weights, -1, keepdims=True)
            probs = (weights * (1.0 / total)).astype(BF16)
            outs.append(dot_nn(probs, v))
            sums.append(peak + jnp.log(total))
        mix[here, :] = jnp.where(lane < HEAD_SIZE, outs[0], outs[1])
        lse_ref[here, :] = jnp.where(lane < HEAD_SIZE, sums[0], sums[1])

    def spread(j, _):
        for h in range(2):
            place = pl.multiple_of(offs[2 * j + h], half)
            there = pl.ds(pl.multiple_of(j * block + h * half, half), half)
            mixed_ref[there, :] = mix[pl.ds(place, half), :].astype(BF16)
        return 0

    lax.fori_loop(0, rows // block, spread, 0)


def attention_backward_kernel(
    offs,
    grads,
    mixed,
    weight,
    normed_ref,
    qkv_ref,
    lse_ref,
    cos_ref,
    sin_ref,
    back_ref,
    wgrad_ref,
    gm,
    delta,
    dq,
    dk,
    dv,
    packed,
):
    rows = grads.shape[0]
    block = 128
    half = block // 2
    tile = 256
    lane_half = lax.broadcasted_iota(jnp.int32, (half, 128), 1)

    def collect(j, _):
        for h in range(2):
            place = pl.multiple_of(offs[2 * j + h], half)
            there = pl.ds(pl.multiple_of(j * block + h * half, half), half)
            g = grads[there, :].astype(F32)
            gm[pl.ds(place, half), :] = g
            product = g * mixed[there, :].astype(F32)
            first = jnp.sum(jnp.where(lane_half < HEAD_SIZE, product, 0.0), -1, keepdims=True)
            second = jnp.sum(jnp.where(lane_half < HEAD_SIZE, 0.0, product), -1, keepdims=True)
            delta[pl.ds(place, half), :] = jnp.where(lane_half < HEAD_SIZE, first, second)
        return 0

    lax.fori_loop(0, rows // block, collect, 0)
    dk[...] = jnp.zeros_like(dk)
    dv[...] = jnp.zeros_like(dv)
    lane = lax.broadcasted_iota(jnp.int32, (tile, 128), 1)
    for i in range(rows // tile):
        width = (i + 1) * tile
        here = slice(i * tile, (i + 1) * tile)
        q = qkv_ref[here, 0:128]
        g = gm[here, :].astype(BF16)
        k, v = qkv_ref[0:width, 128:256], qkv_ref[0:width, 256:384]
        row = lax.broadcasted_iota(jnp.int32, (tile, width), 0) + i * tile
        col = lax.broadcasted_iota(jnp.int32, (tile, width), 1)
        outs = []
        for h in range(2):
            mask = (lane < HEAD_SIZE) if h == 0 else (lane >= HEAD_SIZE)
            at = h * HEAD_SIZE
            q_h = jnp.where(mask, q, jnp.zeros_like(q))
            g_h = jnp.where(mask, g, jnp.zeros_like(g))
            scores = dot_nt(q_h, k)
            scores = jnp.where(col <= row, scores, -jnp.inf)
            probs = jnp.exp(scores - lse_ref[here, at : at + 1])
            slope = dot_nt(g_h, v) - delta[here, at : at + 1]
            grad_scores = (probs * slope).astype(BF16)
            outs.append(dot_nn(grad_scores, k))
            dk[0:width, :] += dot_tn(grad_scores, q_h)
            dv[0:width, :] += dot_tn(probs.astype(BF16), g_h)
        dq[here, :] = jnp.where(lane < HEAD_SIZE, outs[0], outs[1]) * HEAD_SIZE ** (-0.5)

    def unrotate(i, _):
        here = pl.ds(pl.multiple_of(i * tile, tile), tile)
        c, s = cos_ref[here, :], sin_ref[here, :]
        q = dq[here, :]
        k = dk[here, :] + pltpu.roll(dk[here, :], HEAD_SIZE, 1)
        v = dv[here, :] + pltpu.roll(dv[here, :], HEAD_SIZE, 1)
        packed[here, 0:128] = (q * c - swap_halves(q) * s).astype(BF16)
        k = k * c - swap_halves(k) * s
        packed[here, 128:256] = jnp.where(lane < HEAD_SIZE, k, v).astype(BF16)
        return 0

    lax.fori_loop(0, rows // tile, unrotate, 0)
    slab = 256
    for d in range(MODEL_WIDTH // slab):
        cut = slice(d * slab, (d + 1) * slab)
        wgrad_ref[cut, :] = dot_tn(normed_ref[:, cut], packed[...])

    def send(j, _):
        for h in range(2):
            place = pl.multiple_of(offs[2 * j + h], half)
            there = pl.ds(pl.multiple_of(j * block + h * half, half), half)
            back_ref[there, :] = dot_nt(packed[pl.ds(place, half), :], weight[...]).astype(BF16)
        return 0

    lax.fori_loop(0, rows // block, send, 0)


def experts_kernel(
    where_am_i,
    rows_ref,
    cots_ref,
    g0,
    g1,
    g2,
    g3,
    u0,
    u1,
    u2,
    u3,
    d0,
    d1,
    d2,
    d3,
    out_ref,
    back_ref,
    gg0,
    gg1,
    gg2,
    gg3,
    ug0,
    ug1,
    ug2,
    ug3,
    dg0,
    dg1,
    dg2,
    dg3,
    picks,
    slot_gates,
    rows,
    cots,
    outs,
    backs,
):
    e = pl.program_id(0)
    local = pl.num_programs(0)
    blocks = rows.shape[0]
    slots = rows.shape[2]
    first_expert = where_am_i[0]
    fsdp = where_am_i[1]
    slab = MODEL_WIDTH // 4
    every = slots * rows.shape[1]

    def cut(k):
        return pl.ds(pl.multiple_of(lax.bitwise_xor(fsdp, k) * slab, slab), slab)

    @pl.when(e == 0)
    def _():
        def dispatch(j, _):
            here = pl.ds(pl.multiple_of(j * 128, 128), 128)
            marks = cots_ref[here, MODEL_WIDTH : MODEL_WIDTH + 128]
            marks_f = marks.astype(F32)
            lane = lax.broadcasted_iota(jnp.int32, (128, 128), 1)
            slot = lax.broadcasted_iota(jnp.int32, (128, every), 1)
            rank = jnp.zeros((128, every), F32)
            for x in range(every // slots):
                column = jnp.sum(
                    jnp.where(lane == first_expert + x, marks_f, 0.0), -1, keepdims=True
                )
                rank = jnp.where(slot // slots == x, column, rank)
            pick = jnp.where(rank == (slot % slots).astype(F32), 1.0, 0.0).astype(BF16)
            picks[j] = pick
            chosen = dot_tn(pick, marks)
            lane_s = lax.broadcasted_iota(jnp.int32, (every, 128), 1)
            owner = first_expert + lax.broadcasted_iota(jnp.int32, (every, 128), 0) // slots
            wanted = (lane_s >= NE) & (lane_s % NE == owner)
            gate = jnp.sum(jnp.where(wanted, chosen, 0.0), -1, keepdims=True)
            gates = jnp.broadcast_to(gate, (every, 128))
            for x in range(every // slots):
                slot_gates[j, x] = gates[x * slots : (x + 1) * slots]
            for k in range(4):
                to = slice(k * slab, (k + 1) * slab)
                r = dot_tn(pick, rows_ref[here, cut(k)]).astype(BF16)
                c = (dot_tn(pick, cots_ref[here, cut(k)]) * gate).astype(BF16)
                for x in range(every // slots):
                    rows[j, x, :, to] = r[x * slots : (x + 1) * slots]
                    cots[j, x, :, to] = c[x * slots : (x + 1) * slots]
            return 0

        lax.fori_loop(0, blocks, dispatch, 0)

    count = blocks * slots
    gates, ups, downs = (g0, g1, g2, g3), (u0, u1, u2, u3), (d0, d1, d2, d3)
    own_rows = rows[:, e].reshape(count, MODEL_WIDTH)
    own_cots = cots[:, e].reshape(count, MODEL_WIDTH)
    pre_gate = pre_up = grad_hidden = None
    for k in range(4):
        to = slice(k * slab, (k + 1) * slab)
        a = dot_nn(own_rows[:, to], gates[k][0])
        b = dot_nn(own_rows[:, to], ups[k][0])
        c = dot_nt(own_cots[:, to], downs[k][0])
        pre_gate = a if k == 0 else pre_gate + a
        pre_up = b if k == 0 else pre_up + b
        grad_hidden = c if k == 0 else grad_hidden + c
    sigmoid = 1.0 / (1.0 + jnp.exp(-pre_gate))
    silu = pre_gate * sigmoid
    hidden = (silu * pre_up).astype(BF16)
    grad_gate = (grad_hidden * pre_up * sigmoid * (1.0 + pre_gate * (1.0 - sigmoid))).astype(BF16)
    grad_up = (grad_hidden * silu).astype(BF16)
    gate = slot_gates[:, e].reshape(count, 128)[:, 0:1]
    for k in range(4):
        to = slice(k * slab, (k + 1) * slab)
        out = (dot_nn(hidden, downs[k][0]) * gate).astype(BF16)
        back = (dot_nt(grad_gate, gates[k][0]) + dot_nt(grad_up, ups[k][0])).astype(BF16)
        outs[:, e, :, to] = out.reshape(blocks, slots, slab)
        backs[:, e, :, to] = back.reshape(blocks, slots, slab)
        (gg0, gg1, gg2, gg3)[k][0] = dot_tn(own_rows[:, to], grad_gate).astype(BF16)
        (ug0, ug1, ug2, ug3)[k][0] = dot_tn(own_rows[:, to], grad_up).astype(BF16)
        (dg0, dg1, dg2, dg3)[k][0] = dot_tn(hidden, own_cots[:, to]).astype(BF16)

    @pl.when(e == local - 1)
    def _():
        def combine(j, _):
            here = pl.ds(pl.multiple_of(j * 128, 128), 128)
            pick = picks[j]
            for k in range(4):
                to = slice(k * slab, (k + 1) * slab)
                out_ref[here, cut(k)] = dot_nn(
                    pick, outs[j, :, :, to].reshape(every, slab)
                ).astype(BF16)
                back_ref[here, cut(k)] = dot_nn(
                    pick, backs[j, :, :, to].reshape(every, slab)
                ).astype(BF16)
            return 0

        lax.fori_loop(0, blocks, combine, 0)


def whole(shape, dtype):
    return jax.ShapeDtypeStruct(shape, dtype)


def in_vmem(count):
    return [pl.BlockSpec(memory_space=pltpu.VMEM)] * count


def attention_forward(offs, tok, weight, gain, cos, sin):
    n = tok.shape[0]
    return pl.pallas_call(
        attention_forward_kernel,
        out_shape=(
            whole((n, 128), BF16),
            whole((n, MODEL_WIDTH), BF16),
            whole((n, 384), BF16),
            whole((n, 128), F32),
        ),
        in_specs=[pl.BlockSpec(memory_space=pltpu.SMEM)] + in_vmem(5),
        out_specs=tuple(in_vmem(4)),
        scratch_shapes=[pltpu.VMEM((n, 384), F32), pltpu.VMEM((n, 128), F32)],
        compiler_params=pltpu.CompilerParams(vmem_limit_bytes=VMEM_LIMIT),
        cost_estimate=pl.CostEstimate(
            flops=2 * n * MODEL_WIDTH * 384 + 4 * n * n * 128,
            bytes_accessed=n * MODEL_WIDTH * 8,
            transcendentals=n * n,
        ),
        name="attention_forward",
    )(offs, tok, weight, gain, cos, sin)


def attention_backward(offs, grads, mixed, weight, normed, qkv, lse, cos, sin):
    n = grads.shape[0]
    return pl.pallas_call(
        attention_backward_kernel,
        out_shape=(whole((n, MODEL_WIDTH), BF16), whole((MODEL_WIDTH, 256), F32)),
        in_specs=[pl.BlockSpec(memory_space=pltpu.SMEM)] + in_vmem(8),
        out_specs=tuple(in_vmem(2)),
        scratch_shapes=[pltpu.VMEM((n, 128), F32) for _ in range(5)]
        + [pltpu.VMEM((n, 256), BF16)],
        compiler_params=pltpu.CompilerParams(vmem_limit_bytes=VMEM_LIMIT),
        cost_estimate=pl.CostEstimate(
            flops=4 * n * MODEL_WIDTH * 256 + 10 * n * n * 128,
            bytes_accessed=n * MODEL_WIDTH * 8,
            transcendentals=n * n,
        ),
        name="attention_backward",
    )(offs, grads, mixed, weight, normed, qkv, lse, cos, sin)


def run_experts(where_am_i, rows, cots, gates, ups, downs):
    n = rows.shape[0]
    local, slab, hidden = gates[0].shape
    blocks = n // 128
    once = pl.Buffered(1)

    def fixed(shape):
        return pl.BlockSpec(shape, lambda e: (0, 0), pipeline_mode=once)

    def per_expert(shape):
        return pl.BlockSpec((1,) + shape, lambda e: (e, 0, 0))

    wide, tall = (slab, hidden), (hidden, slab)
    results = pl.pallas_call(
        experts_kernel,
        grid=(local,),
        out_shape=[whole((n, MODEL_WIDTH), BF16)] * 2
        + [whole((local,) + wide, BF16)] * 8
        + [whole((local,) + tall, BF16)] * 4,
        in_specs=[
            pl.BlockSpec(memory_space=pltpu.SMEM),
            fixed((n, MODEL_WIDTH)),
            fixed((n, MODEL_WIDTH + 128)),
        ]
        + [per_expert(wide)] * 8
        + [per_expert(tall)] * 4,
        out_specs=[fixed((n, MODEL_WIDTH))] * 2
        + [per_expert(wide)] * 8
        + [per_expert(tall)] * 4,
        scratch_shapes=[
            pltpu.VMEM((blocks, 128, local * CAP), BF16),
            pltpu.VMEM((blocks, local, CAP, 128), F32),
        ]
        + [pltpu.VMEM((blocks, local, CAP, MODEL_WIDTH), BF16)] * 4,
        compiler_params=pltpu.CompilerParams(
            vmem_limit_bytes=VMEM_LIMIT, dimension_semantics=("arbitrary",)
        ),
        cost_estimate=pl.CostEstimate(
            flops=18 * local * blocks * CAP * MODEL_WIDTH * hidden,
            bytes_accessed=24 * local * MODEL_WIDTH * hidden,
            transcendentals=local * blocks * CAP * hidden,
        ),
        name="experts",
    )(where_am_i, rows, cots, *gates, *ups, *downs)
    return results[0], results[1], results[2:6], results[6:10], results[10:14]


def after(x, *others):
    return lax.optimization_barrier((x,) + others)[0]


def heads_body(
    tokens,
    routes,
    route_gates,
    first_gain,
    query_weight,
    key_weight,
    value_matrix,
    output_weight,
    second_gain,
    expert_gate,
    expert_up,
    expert_down,
    cotangent,
):
    n = lax.axis_size("ctx")
    c, f = lax.axis_index("ctx"), lax.axis_index("fsdp")
    local = expert_gate.shape[0]
    rows = tokens.shape[1]
    length = rows * n
    half = rows // 2
    slice_rows = query_weight.shape[0]
    order = jnp.array(ring_order(n), jnp.int32)
    p = jnp.sum(jnp.where(order == c, jnp.arange(n, dtype=jnp.int32), 0))
    ahead = order[(p + jnp.arange(n, dtype=jnp.int32)) % n]

    x_own, cot_own = tokens[0], cotangent[0]
    tok = jnp.concatenate(ring_gather(x_own, n), 0)

    gains = jnp.pad(jnp.stack([first_gain, second_gain], 1), ((0, 0), (0, 126)))
    by_head = jnp.concatenate(
        [
            query_weight.reshape(slice_rows, n, 128),
            key_weight.reshape(slice_rows, n, 64),
            value_matrix.reshape(slice_rows, n, 64),
            jnp.broadcast_to(gains[:, None, :], (slice_rows, n, 128)),
        ],
        2,
    ).transpose(1, 0, 2)
    assembled = jnp.zeros((n, slice_rows, 384), BF16)
    for j in range(n):
        block = lax.dynamic_index_in_dim(by_head, ahead[j], 0, keepdims=True)
        if j:
            block = shift(block, n, j)
        assembled = lax.dynamic_update_slice(assembled, block, (ahead[(n - j) % n], 0, 0))
    weight_full = jnp.zeros((n, 4, slice_rows, 384), BF16)
    for k, piece in enumerate(swap_gather(assembled)):
        weight_full = lax.dynamic_update_slice(weight_full, piece[:, None], (0, f ^ k, 0, 0))
    weight_full = weight_full.reshape(MODEL_WIDTH, 384)
    weight = weight_full[:, 0:256]
    wide_weight = jnp.concatenate(
        [
            weight_full[:, 0:128],
            weight_full[:, 128:192],
            weight_full[:, 128:192],
            weight_full[:, 192:256],
            weight_full[:, 192:256],
        ],
        1,
    )
    gain_rows = weight_full[:, 256:264].astype(F32).T
    gain_one, gain_two = gain_rows[0:1], gain_rows[1:2]

    out_slices = jnp.stack(ring_gather(output_weight, n), 0)
    out_full = jnp.zeros((n, 4, slice_rows, MODEL_WIDTH), BF16)
    for k, piece in enumerate(swap_gather(out_slices)):
        out_full = lax.dynamic_update_slice(out_full, piece[:, None], (0, f ^ k, 0, 0))
    out_full = out_full.reshape(n, 128, MODEL_WIDTH)

    gates = swap_gather(after(expert_gate, weight_full))
    ups = swap_gather(after(expert_up, gates[2]))
    downs = swap_gather(after(expert_down, ups[2]))

    hits = routes[0][:, :, None] == jnp.arange(NE, dtype=jnp.int32)
    gate_table = jnp.sum(jnp.where(hits, route_gates[0][:, :, None], 0.0), 1)
    hit = jnp.any(hits, 1)
    earlier = jnp.tril(jnp.ones((rows, rows), F32), -1).astype(BF16)
    rank = jnp.dot(earlier, hit.astype(BF16), preferred_element_type=F32)
    rank = jnp.where(hit, rank, -1.0)
    top = lax.reduce_precision(gate_table, 8, 7)
    rest = gate_table - top
    middle = lax.reduce_precision(rest, 8, 7)
    marks = jnp.concatenate([rank, top, middle, rest - middle], 1).astype(BF16)
    cots = ring_gather(after(jnp.concatenate([cot_own, marks], 1), tok), n)
    cots = jnp.concatenate(cots, 0)

    half_index = jnp.arange(2, dtype=jnp.int32)[None, :]
    offs = (
        jnp.where(half_index == 0, ahead[:, None], 2 * n - 1 - ahead[:, None]) * half
    ).reshape(-1)
    freqs = ROPE_BASE ** (-jnp.arange(0, HEAD_SIZE, 2, dtype=jnp.float32) / HEAD_SIZE)
    angles = jnp.arange(length, dtype=jnp.float32)[:, None] * jnp.tile(freqs, 4)[None, :]
    cos_table = jnp.cos(angles)
    signs = jnp.where(jnp.arange(128) % HEAD_SIZE < HEAD_SIZE // 2, -1.0, 1.0)
    sin_table = jnp.sin(angles) * signs[None, :]
    mixed_heads, normed_one, qkv, lse = attention_forward(
        offs, tok, wide_weight, gain_one, cos_table, sin_table
    )

    mixed = jnp.concatenate(
        [
            shift(mixed_heads[j * rows : (j + 1) * rows], n, j) if j else mixed_heads[:rows]
            for j in range(n)
        ],
        1,
    )
    out_behind = jnp.concatenate([out_full[(n - j) % n] for j in range(n)], 0)
    residual = x_own.astype(F32) + jnp.dot(mixed, out_behind, preferred_element_type=F32)
    scale_two = lax.rsqrt(jnp.mean(residual * residual, -1, keepdims=True) + EPSILON)
    unit_two = residual * scale_two
    normed_two = (unit_two * gain_two).astype(BF16)

    all_rows = jnp.concatenate(ring_gather(normed_two, n), 0)
    where_am_i = jnp.stack([c * local, f]).astype(jnp.int32)
    out_part, back_part, gate_grads, up_grads, down_grads = run_experts(
        where_am_i, all_rows, cots, gates, ups, downs
    )
    grad_two = ring_scatter([back_part[j * rows : (j + 1) * rows] for j in range(n)], n)
    out_part = after(out_part, grad_two)
    expert_sum = ring_scatter([out_part[j * rows : (j + 1) * rows] for j in range(n)], n)
    block_output = (residual + expert_sum).astype(BF16)
    gate_shard = swap_scatter(gate_grads)
    up_shard = swap_scatter([after(g, gate_shard) for g in up_grads])
    down_shard = swap_scatter([after(g, up_shard) for g in down_grads])

    upstream = cot_own.astype(F32)
    second_part = jnp.sum(grad_two * unit_two, 0)
    scaled_two = grad_two * gain_two
    grad_residual = upstream + scale_two * (
        scaled_two - unit_two * jnp.mean(scaled_two * unit_two, -1, keepdims=True)
    )
    grad_resid_b = grad_residual.astype(BF16)
    out_all = out_full.reshape(n * 128, MODEL_WIDTH)
    grad_mixed = lax.dot_general(
        grad_resid_b, out_all, (((1,), (1,)), ((), ())), preferred_element_type=F32
    ).astype(BF16)
    grad_heads = [
        shift(grad_mixed[:, i * 128 : (i + 1) * 128], n, i) if i else grad_mixed[:, :128]
        for i in range(n)
    ]
    grad_heads = jnp.concatenate([grad_heads[(n - j) % n] for j in range(n)], 0)
    back_tokens, weight_grad = attention_backward(
        offs, grad_heads, mixed_heads, weight, normed_one, qkv, lse, cos_table, sin_table
    )

    output_part = lax.dot_general(
        mixed, grad_resid_b, (((0,), (0,)), ((), ())), preferred_element_type=F32
    ).astype(BF16)
    output_part = output_part.reshape(n, 4, slice_rows, MODEL_WIDTH)
    output_slices = swap_scatter(
        [lax.dynamic_index_in_dim(output_part, f ^ k, 1, keepdims=False) for k in range(4)]
    ).astype(BF16)
    output_shard = ring_scatter([output_slices[(n - j) % n] for j in range(n)], n)

    total = second_part.reshape(8, 128)
    bit = 1
    while bit < n:
        total = total + lax.ppermute(total, "ctx", [(i, i ^ bit) for i in range(n)])
        bit *= 2
    for bit in (1, 2):
        total = total + swap(total, bit)
    device = c * 4 + f
    second_shard = lax.dynamic_slice(total.reshape(-1), (device * slice_rows,), (slice_rows,))

    first_part = jnp.sum(weight_grad * weight.astype(F32), -1, keepdims=True) / gain_one.T
    weight_grad = jnp.concatenate(
        [weight_grad, jnp.broadcast_to(first_part, (MODEL_WIDTH, 128))], 1
    ).astype(BF16)
    weight_grad = weight_grad.reshape(n, 4, slice_rows, 384)
    weight_rows = swap_scatter(
        [lax.dynamic_index_in_dim(weight_grad, f ^ k, 1, keepdims=False) for k in range(4)]
    ).astype(BF16)
    heads_back = jnp.zeros((n, slice_rows, 384), BF16)
    for j in range(n):
        block = lax.dynamic_index_in_dim(weight_rows, ahead[j], 0, keepdims=True)
        if j:
            block = shift(block, n, j)
        heads_back = lax.dynamic_update_slice(heads_back, block, (ahead[(n - j) % n], 0, 0))
    heads_back = heads_back.astype(F32)
    query_shard = heads_back[:, :, 0:128].transpose(1, 0, 2).reshape(slice_rows, n * 128)
    key_shard = heads_back[:, :, 128:192].transpose(1, 0, 2).reshape(slice_rows, n * 64)
    value_shard = heads_back[:, :, 192:256].transpose(1, 0, 2).reshape(slice_rows, n * 64)
    first_shard = jnp.sum(heads_back[:, :, 256], 0)

    grad_one = ring_scatter([back_tokens[j * rows : (j + 1) * rows] for j in range(n)], n)
    inputs = x_own.astype(F32)
    scale_one = lax.rsqrt(jnp.mean(inputs * inputs, -1, keepdims=True) + EPSILON)
    unit_one = inputs * scale_one
    scaled_one = grad_one * gain_one
    input_grad = grad_residual + scale_one * (
        scaled_one - unit_one * jnp.mean(scaled_one * unit_one, -1, keepdims=True)
    )
    return (
        block_output[None],
        input_grad[None],
        first_shard,
        query_shard,
        key_shard,
        value_shard,
        output_shard,
        second_shard,
        gate_shard,
        up_shard,
        down_shard,
    )


def positions(index, count_of_rows, ctx_count):
    block = index // count_of_rows
    local = index % count_of_rows
    half = count_of_rows // 2
    return jnp.where(
        local < half, block * half + local, (2 * ctx_count - 1 - block) * half + local - half
    )


def rotary(places):
    freqs = ROPE_BASE ** (-jnp.arange(0, HEAD_SIZE, 2, dtype=jnp.float32) / HEAD_SIZE)
    angles = places.astype(jnp.float32)[:, None] * freqs[None, :]
    return (jnp.cos(angles), jnp.sin(angles))


def apply_rotation(values, cosine_table, sine_table):
    half = values.shape[-1] // 2
    first = values[..., :half]
    second = values[..., half:]
    cos_part = cosine_table[:, None, :]
    sin_part = sine_table[:, None, :]
    return jnp.concatenate(
        [first * cos_part - second * sin_part, second * cos_part + first * sin_part], -1
    )


def half_pieces(array, axis):
    width = array.shape[axis] // 2
    return [
        lax.slice_in_dim(array, half_index * width, (half_index + 1) * width, axis=axis)
        for half_index in range(2)
    ]


def attend(queries, key_block, value_block, allowed):
    scores = jnp.einsum(
        "qhgd,khd->hgqk", queries, key_block, preferred_element_type=jnp.float32
    ) * HEAD_SIZE ** (-0.5)
    scores = jnp.where(allowed[None, None], scores, -jnp.inf)
    row_peak = jnp.max(scores, -1, keepdims=True)
    logsum = row_peak + jnp.log(jnp.sum(jnp.exp(scores - row_peak), -1, keepdims=True))
    prob_rows = jnp.exp(scores - logsum).astype(jnp.bfloat16)
    rows_mixed = jnp.einsum(
        "hgqk,khd->qhgd", prob_rows, value_block, preferred_element_type=jnp.float32
    )
    return (rows_mixed, logsum[..., 0])


def attend_back(queries, key_block, value_block, grad_block, logsum, rows_of_delta, allowed):
    scores = jnp.einsum(
        "qhgd,khd->hgqk", queries, key_block, preferred_element_type=jnp.float32
    ) * HEAD_SIZE ** (-0.5)
    scores = jnp.where(allowed[None, None], scores, -jnp.inf)
    prob_rows = jnp.exp(scores - logsum[..., None])
    grad_probs = jnp.einsum(
        "qhgd,khd->hgqk", grad_block, value_block, preferred_element_type=jnp.float32
    )
    grad_scores = (prob_rows * (grad_probs - rows_of_delta[..., None])).astype(jnp.bfloat16)
    results = []
    results.append(
        jnp.einsum("hgqk,khd->qhgd", grad_scores, key_block, preferred_element_type=jnp.float32)
        * HEAD_SIZE ** (-0.5)
    )
    results.append(
        jnp.einsum("hgqk,qhgd->khd", grad_scores, queries, preferred_element_type=jnp.float32)
        * HEAD_SIZE ** (-0.5)
    )
    results.append(
        jnp.einsum(
            "hgqk,qhgd->khd",
            prob_rows.astype(jnp.bfloat16),
            grad_block,
            preferred_element_type=jnp.float32,
        )
    )
    return results


def body(
    tokens,
    routes,
    route_gates,
    first_gain,
    query_weight,
    key_weight,
    value_matrix,
    output_weight,
    second_gain,
    expert_gate,
    expert_up,
    expert_down,
    cotangent,
):
    count_of_rows = tokens.shape[1]
    ctx_count = lax.axis_size("ctx")
    head_groups = QUERY_HEADS // KEY_VALUE_HEADS
    sequence_length = count_of_rows * ctx_count
    gain_one, full_query, full_key, full_value, full_output, gain_two = (
        lax.all_gather(first_gain, ("ctx", "fsdp"), axis=0, tiled=True),
        lax.all_gather(query_weight, ("ctx", "fsdp"), axis=0, tiled=True),
        lax.all_gather(key_weight, ("ctx", "fsdp"), axis=0, tiled=True),
        lax.all_gather(value_matrix, ("ctx", "fsdp"), axis=0, tiled=True),
        lax.all_gather(output_weight, ("ctx", "fsdp"), axis=0, tiled=True),
        lax.all_gather(second_gain, ("ctx", "fsdp"), axis=0, tiled=True),
    )
    gate_full, up_full, down_full = (
        lax.all_gather(expert_gate, "fsdp", axis=1, tiled=True),
        lax.all_gather(expert_up, "fsdp", axis=1, tiled=True),
        lax.all_gather(expert_down, "fsdp", axis=2, tiled=True),
    )
    gain_first = gain_one.astype(jnp.float32)
    gain_second = gain_two.astype(jnp.float32)
    own_places = positions(
        lax.axis_index("ctx") * count_of_rows + jnp.arange(count_of_rows, dtype=jnp.int32),
        count_of_rows,
        ctx_count,
    )
    all_places = positions(jnp.arange(sequence_length, dtype=jnp.int32), count_of_rows, ctx_count)
    cosine_table, sine_table = rotary(own_places)
    allowed = all_places[None, :] <= own_places[:, None]
    inputs = tokens[0].astype(jnp.float32)
    scale_one = lax.rsqrt(jnp.mean(inputs * inputs, -1, keepdims=True) + EPSILON)
    unit_one = inputs * scale_one
    normed_one = (unit_one * gain_first).astype(jnp.bfloat16)
    rows_of_query = jnp.dot(normed_one, full_query, preferred_element_type=jnp.float32)
    rows_of_key = jnp.dot(normed_one, full_key, preferred_element_type=jnp.float32)
    rows_of_value = jnp.dot(normed_one, full_value, preferred_element_type=jnp.float32)
    rotated_query = apply_rotation(
        rows_of_query.reshape(count_of_rows, QUERY_HEADS, HEAD_SIZE), cosine_table, sine_table
    ).astype(jnp.bfloat16)
    rotated_key = (
        apply_rotation(
            rows_of_key.reshape(count_of_rows, KEY_VALUE_HEADS, HEAD_SIZE), cosine_table, sine_table
        )
        .astype(jnp.bfloat16)
        .reshape(count_of_rows, KEY_VALUE_HEADS * HEAD_SIZE)
    )
    value_flat = rows_of_value.astype(jnp.bfloat16)
    every_key, every_value = (
        lax.all_gather(rotated_key, "ctx", axis=0, tiled=True),
        lax.all_gather(value_flat, "ctx", axis=0, tiled=True),
    )
    query_portions = half_pieces(
        rotated_query.reshape(count_of_rows, KEY_VALUE_HEADS, head_groups, HEAD_SIZE), 1
    )
    key_portions = half_pieces(every_key.reshape(sequence_length, KEY_VALUE_HEADS, HEAD_SIZE), 1)
    value_portions = half_pieces(
        every_value.reshape(sequence_length, KEY_VALUE_HEADS, HEAD_SIZE), 1
    )
    results = [
        attend(
            query_portions[half_index],
            key_portions[half_index],
            value_portions[half_index],
            allowed,
        )
        for half_index in range(2)
    ]
    rows_mixed = (
        jnp.concatenate([result_pair[0] for result_pair in results], 1)
        .reshape(count_of_rows, QUERY_HEADS * HEAD_SIZE)
        .astype(jnp.bfloat16)
    )
    logsum = jnp.concatenate([result_pair[1] for result_pair in results], 0)
    residual = inputs + jnp.dot(rows_mixed, full_output, preferred_element_type=jnp.float32)
    scale_two = lax.rsqrt(jnp.mean(residual * residual, -1, keepdims=True) + EPSILON)
    unit_two = residual * scale_two
    normed_two = (unit_two * gain_second).astype(jnp.bfloat16)
    upstream = cotangent[0].astype(jnp.float32)
    route_flat = routes[0].reshape(-1)
    weight_rows = route_gates[0]
    owners = jnp.arange(count_of_rows * TOPK, dtype=jnp.int32) // TOPK
    one_hot = (route_flat[:, None] == jnp.arange(NE, dtype=jnp.int32)[None, :]).astype(jnp.int32)
    slot_index = route_flat * CAP + jnp.sum((jnp.cumsum(one_hot, 0) - 1) * one_hot, 1)
    send_rows = (
        jnp.zeros((NE * CAP, MODEL_WIDTH), jnp.bfloat16)
        .at[slot_index]
        .set(normed_two[owners])
        .reshape(NE, CAP, MODEL_WIDTH)
    )
    route_cot = (weight_rows.reshape(-1)[:, None] * upstream[owners]).astype(jnp.bfloat16)
    send_grads = (
        jnp.zeros((NE * CAP, MODEL_WIDTH), jnp.bfloat16)
        .at[slot_index]
        .set(route_cot)
        .reshape(NE, CAP, MODEL_WIDTH)
    )
    arrived_rows, arrived_grads = (
        lax.all_to_all(send_rows, "ctx", split_axis=0, concat_axis=1, tiled=True),
        lax.all_to_all(send_grads, "ctx", split_axis=0, concat_axis=1, tiled=True),
    )
    pre_gate = jnp.einsum(
        "esd,edf->esf", arrived_rows, gate_full, preferred_element_type=jnp.float32
    )
    pre_up = jnp.einsum("esd,edf->esf", arrived_rows, up_full, preferred_element_type=jnp.float32)
    sigmoid_gate = jax.nn.sigmoid(pre_gate)
    silu_gate = pre_gate * sigmoid_gate
    hidden = (silu_gate * pre_up).astype(jnp.bfloat16)
    expert_out = jnp.einsum(
        "esf,efd->esd", hidden, down_full, preferred_element_type=jnp.float32
    ).astype(jnp.bfloat16)
    grad_hidden = jnp.einsum(
        "esd,efd->esf", arrived_grads, down_full, preferred_element_type=jnp.float32
    )
    down_grad = jnp.einsum(
        "esf,esd->efd", hidden, arrived_grads, preferred_element_type=jnp.float32
    )
    grad_pre_gate = (
        grad_hidden * pre_up * sigmoid_gate * (1.0 + pre_gate * (1.0 - sigmoid_gate))
    ).astype(jnp.bfloat16)
    grad_pre_up = (grad_hidden * silu_gate).astype(jnp.bfloat16)
    gate_grad = jnp.einsum(
        "esd,esf->edf", arrived_rows, grad_pre_gate, preferred_element_type=jnp.float32
    )
    up_grad = jnp.einsum(
        "esd,esf->edf", arrived_rows, grad_pre_up, preferred_element_type=jnp.float32
    )
    back_rows = (
        jnp.einsum("esf,edf->esd", grad_pre_gate, gate_full, preferred_element_type=jnp.float32)
        + jnp.einsum("esf,edf->esd", grad_pre_up, up_full, preferred_element_type=jnp.float32)
    ).astype(jnp.bfloat16)
    returned_out, returned_grads = (
        lax.all_to_all(expert_out, "ctx", split_axis=1, concat_axis=0, tiled=True),
        lax.all_to_all(back_rows, "ctx", split_axis=1, concat_axis=0, tiled=True),
    )
    gate_shard, up_shard, down_shard = (
        lax.psum_scatter(
            gate_grad.astype(jnp.bfloat16), "fsdp", scatter_dimension=1, tiled=True
        ).astype(jnp.float32),
        lax.psum_scatter(
            up_grad.astype(jnp.bfloat16), "fsdp", scatter_dimension=1, tiled=True
        ).astype(jnp.float32),
        lax.psum_scatter(
            down_grad.astype(jnp.bfloat16), "fsdp", scatter_dimension=2, tiled=True
        ).astype(jnp.float32),
    )
    picked_out = (
        returned_out.reshape(NE * CAP, MODEL_WIDTH)[slot_index]
        .astype(jnp.float32)
        .reshape(count_of_rows, TOPK, MODEL_WIDTH)
    )
    expert_sum = jnp.sum(weight_rows[:, :, None] * picked_out, 1)
    block_output = (residual + expert_sum).astype(jnp.bfloat16)
    grad_two = jnp.sum(
        returned_grads.reshape(NE * CAP, MODEL_WIDTH)[slot_index]
        .astype(jnp.float32)
        .reshape(count_of_rows, TOPK, MODEL_WIDTH),
        1,
    )
    second_part = jnp.sum(grad_two * unit_two, 0)
    scaled_two = grad_two * gain_second
    grad_residual = upstream + scale_two * (
        scaled_two - unit_two * jnp.mean(scaled_two * unit_two, -1, keepdims=True)
    )
    grad_resid_b = grad_residual.astype(jnp.bfloat16)
    output_part = jnp.dot(rows_mixed.T, grad_resid_b, preferred_element_type=jnp.float32)
    mixed_gradient = jnp.dot(
        grad_resid_b, full_output.T, preferred_element_type=jnp.float32
    ).astype(jnp.bfloat16)
    gradient_heads = mixed_gradient.reshape(count_of_rows, KEY_VALUE_HEADS, head_groups, HEAD_SIZE)
    rows_of_delta = jnp.sum(
        gradient_heads.astype(jnp.float32)
        * rows_mixed.reshape(count_of_rows, KEY_VALUE_HEADS, head_groups, HEAD_SIZE).astype(
            jnp.float32
        ),
        -1,
    ).transpose(1, 2, 0)
    grad_parts = half_pieces(gradient_heads, 1)
    logsum_parts = half_pieces(logsum, 0)
    delta_parts = half_pieces(rows_of_delta, 0)
    pieces = [
        attend_back(
            query_portions[half_index],
            key_portions[half_index],
            value_portions[half_index],
            grad_parts[half_index],
            logsum_parts[half_index],
            delta_parts[half_index],
            allowed,
        )
        for half_index in range(2)
    ]
    grad_query_rot = jnp.concatenate([piece_list[0] for piece_list in pieces], 1)
    key_partial = jnp.concatenate([piece_list[1] for piece_list in pieces], 1).reshape(
        sequence_length, KEY_VALUE_HEADS * HEAD_SIZE
    )
    value_partial = jnp.concatenate([piece_list[2] for piece_list in pieces], 1).reshape(
        sequence_length, KEY_VALUE_HEADS * HEAD_SIZE
    )
    rotated_key_gradient, value_gradient_rows = (
        lax.psum_scatter(
            key_partial.astype(jnp.bfloat16), "ctx", scatter_dimension=0, tiled=True
        ).astype(jnp.float32),
        lax.psum_scatter(
            value_partial.astype(jnp.bfloat16), "ctx", scatter_dimension=0, tiled=True
        ).astype(jnp.float32),
    )
    grad_query = (
        apply_rotation(
            grad_query_rot.reshape(count_of_rows, QUERY_HEADS, HEAD_SIZE), cosine_table, -sine_table
        )
        .reshape(count_of_rows, QUERY_HEADS * HEAD_SIZE)
        .astype(jnp.bfloat16)
    )
    key_gradient = (
        apply_rotation(
            rotated_key_gradient.reshape(count_of_rows, KEY_VALUE_HEADS, HEAD_SIZE),
            cosine_table,
            -sine_table,
        )
        .reshape(count_of_rows, KEY_VALUE_HEADS * HEAD_SIZE)
        .astype(jnp.bfloat16)
    )
    value_gradient = value_gradient_rows.astype(jnp.bfloat16)
    grad_one = (
        jnp.dot(grad_query, full_query.T, preferred_element_type=jnp.float32)
        + jnp.dot(key_gradient, full_key.T, preferred_element_type=jnp.float32)
        + jnp.dot(value_gradient, full_value.T, preferred_element_type=jnp.float32)
    )
    first_part = jnp.sum(grad_one * unit_one, 0)
    scaled_one = grad_one * gain_first
    input_grad = grad_residual + scale_one * (
        scaled_one - unit_one * jnp.mean(scaled_one * unit_one, -1, keepdims=True)
    )
    query_part = jnp.dot(normed_one.T, grad_query, preferred_element_type=jnp.float32)
    key_part = jnp.dot(normed_one.T, key_gradient, preferred_element_type=jnp.float32)
    value_part = jnp.dot(normed_one.T, value_gradient, preferred_element_type=jnp.float32)
    shares = (
        lax.psum_scatter(first_part, ("ctx", "fsdp"), scatter_dimension=0, tiled=True),
        lax.psum_scatter(query_part, ("ctx", "fsdp"), scatter_dimension=0, tiled=True),
        lax.psum_scatter(key_part, ("ctx", "fsdp"), scatter_dimension=0, tiled=True),
        lax.psum_scatter(value_part, ("ctx", "fsdp"), scatter_dimension=0, tiled=True),
        lax.psum_scatter(output_part, ("ctx", "fsdp"), scatter_dimension=0, tiled=True),
        lax.psum_scatter(second_part, ("ctx", "fsdp"), scatter_dimension=0, tiled=True),
    )
    return (
        block_output[None],
        input_grad[None],
        shares[0],
        shares[1],
        shares[2],
        shares[3],
        shares[4],
        shares[5],
        gate_shard,
        up_shard,
        down_shard,
    )


def solution(mesh):
    by_heads = mesh.shape["ctx"] == KEY_VALUE_HEADS and mesh.shape["fsdp"] == 4
    placed = (
        P("fsdp", "ctx", None),
        P("fsdp", "ctx", None),
        P("fsdp", "ctx", None),
        P(("ctx", "fsdp")),
        P(("ctx", "fsdp"), None),
        P(("ctx", "fsdp"), None),
        P(("ctx", "fsdp"), None),
        P(("ctx", "fsdp"), None),
        P(("ctx", "fsdp")),
        P("ctx", "fsdp", None),
        P("ctx", "fsdp", None),
        P("ctx", None, "fsdp"),
        P("fsdp", "ctx", None),
    )
    return jax.shard_map(
        heads_body if by_heads else body,
        mesh=mesh,
        in_specs=placed,
        out_specs=(
            P("fsdp", "ctx", None),
            P("fsdp", "ctx", None),
            P(("ctx", "fsdp")),
            P(("ctx", "fsdp"), None),
            P(("ctx", "fsdp"), None),
            P(("ctx", "fsdp"), None),
            P(("ctx", "fsdp"), None),
            P(("ctx", "fsdp")),
            P("ctx", "fsdp", None),
            P("ctx", "fsdp", None),
            P("ctx", None, "fsdp"),
        ),
        check_vma=False,
    )
```
